32 devices in a mesh: expert: 8 (over z, y), dp: 4 (over x, core).
Axes of the slice: x: 2, y: 2, z: 4, core: 2. Of those that a mesh axis runs over, the one named last changes fastest.
Arguments:
- grad_parts: bfloat16 [4, 8, 3584, 1024], P('dp', 'expert'), may hold values from -6 to 6
- owner_slot: int32 [8], replicated, may hold values from 0 to 7, each once
- slot_expert: int32 [8, 2], replicated, may hold values from 0 to 7, all different within a row
- master: float32 [8, 3584, 1024], P(None, 'expert', 'dp'), may hold values from -1.5 to 1.5
- moment_one: float32 [8, 3584, 1024], P(None, 'expert', 'dp'), may hold values from -2 to 2
- moment_two: float32 [8, 3584, 1024], P(None, 'expert', 'dp'), may hold values from 0.01 to 1
- ema_weights: float32 [8, 3584, 1024], P(None, 'expert', 'dp'), may hold values from -1.5 to 1.5
Outputs:
- master_out: float32 [8, 3584, 1024], P(None, 'expert', 'dp')
- moment_one_out: float32 [8, 3584, 1024], P(None, 'expert', 'dp')
- moment_two_out: float32 [8, 3584, 1024], P(None, 'expert', 'dp')
- ema_out: float32 [8, 3584, 1024], P(None, 'expert', 'dp')
- replicas: bfloat16 [16, 3584, 1024], P('expert', None, 'dp')
The draws below stay inside these ranges and needn't reach their ends.
Inputs may be any that keep to these rules, and one draw needn't show every extreme that they name: `owner_slot`: a permutation of the 8 experts; position k belongs to expert-axis index k. `slot_expert`: each row names 2 different experts, and every expert is named by some row.
All inputs are finite; a program needn't handle non-finite values.
Results may differ from the reference program's by a relative error of at most 0.009.
Values may be sent and summed in bfloat16 or wider, within the bound.
A program may use at most 128 MiB of HBM per device.

```python
import math
import jax
import jax.numpy as jnp
from jax import lax

ROWS = 3584
HIDDEN_SIZE = 1024
SLOTS = 2
STEP = 10
EXPERTS = 8
N_EXPERT = 8
N_DP = 4


def spiked(result, own_key, source, target, parts, factor):
    def block_of(axis_at):
        return (jnp.arange(result.shape[axis_at]) // (result.shape[axis_at] // parts)).reshape((-1,) + (1,) * (result.ndim - 1 - axis_at))

    near = jax.random.permutation(own_key, parts)[block_of(target)]
    second = (block_of(target) + parts // 2) % parts
    return jnp.where((block_of(source) == near) | (block_of(source) == second), factor * result, result)


def shard_levels(rng, dims, pieces, least, high):
    def one(position, shards_of):
        heights = jax.random.uniform(jax.random.fold_in(jax.random.fold_in(rng, 6), position), (shards_of,), jnp.float32, least / len(pieces), high / len(pieces))
        return jnp.repeat(jnp.exp(heights), dims[position] // shards_of).reshape((-1,) + (1,) * (len(dims) - position - 1))

    factor_of = one(*pieces[0])
    for cut in pieces[1:]:
        factor_of = factor_of * one(*cut)
    return factor_of


def choose_distinct(rng, rows, count, top, lift):
    ranking = jax.random.permutation(jax.random.fold_in(rng, 1), count)
    pull = ranking
    for power in range(3):
        pull = pull * pull // count
    pull = pull * lift // count
    tickets = jax.random.randint(jax.random.fold_in(rng, 2), (rows, count), 0, 4096) + pull
    fixed_rows = jax.random.permutation(jax.random.fold_in(rng, 3), rows)[jnp.arange(count) % rows]
    tickets = jnp.where(jnp.arange(rows)[:, None] == fixed_rows[None, :], 1 << 14, tickets)
    priority = tickets * count + jnp.arange(count)
    return lax.top_k(priority.astype(jnp.int32), top)[1].astype(jnp.int32)


def noise(stream_key, dims, scale, most, split=(), kind=jnp.bfloat16):
    drawn = jax.random.normal(stream_key, dims, jnp.float32) * scale
    if len(split) > 0:
        drawn = shard_levels(stream_key, dims, split, -0.22, 0.18) * drawn
    return jnp.clip(drawn, min=-most, max=most).astype(kind)


def gaussian_with(own_key, shape, width, limit, split, heavy, kind=jnp.bfloat16):
    result = width * jax.random.normal(own_key, shape, jnp.float32)
    if split:
        result = result * shard_levels(own_key, shape, split, -0.22, 0.18)
    return jnp.clip(spiked(result, jax.random.fold_in(own_key, 3), *heavy), -limit, limit).astype(kind)


def setup_inputs(seed: int = 0) -> dict:
    seeds = jax.random.split(jax.random.key(seed), 8)
    grad_parts = gaussian_with(seeds[0], (N_DP, EXPERTS, ROWS, HIDDEN_SIZE), 1.0, 6.0, ((0, 4), (1, 8)), (0, 3, 4, 2.0))
    owner_slot = jax.random.permutation(seeds[1], EXPERTS).astype(jnp.int32)
    slot_expert = choose_distinct(seeds[2], N_EXPERT, EXPERTS, SLOTS, 4096)
    master = noise(seeds[3], (EXPERTS, ROWS, HIDDEN_SIZE), 0.25, 1.5, ((1, 8), (2, 4)), jnp.float32)
    moment_one = noise(seeds[4], (EXPERTS, ROWS, HIDDEN_SIZE), 0.3, 2.0, ((1, 8), (2, 4)), jnp.float32)
    moment_two = jnp.clip(jnp.exp(math.log(1.0) - 4.6051702 * jax.random.uniform(seeds[5], (EXPERTS, ROWS, HIDDEN_SIZE), jnp.float32) ** shard_levels(seeds[5], (EXPERTS, ROWS, HIDDEN_SIZE), ((1, 8), (2, 4)), -0.2, 0.2)), 0.01, 1.0)
    ema_weights = noise(seeds[6], (EXPERTS, ROWS, HIDDEN_SIZE), 0.25, 1.5, ((1, 8), (2, 4)), jnp.float32)
    return {"grad_parts": grad_parts, "owner_slot": owner_slot, "slot_expert": slot_expert, "master": master, "moment_one": moment_one, "moment_two": moment_two, "ema_weights": ema_weights}


beta_one = 0.9
beta_two = 0.999
adam_eps = 1e-08
learn_rate = 0.05
decay_rate = 0.1
ema_decay = 0.99

def reference(grad_parts, owner_slot, slot_expert, master, moment_one, moment_two, ema_weights):
    summed = grad_parts[0].astype(jnp.float32)
    for copy_index in range(1, N_DP):
        summed = summed + grad_parts[copy_index].astype(jnp.float32)
    gradient = jnp.take(summed, owner_slot, axis=0)
    correct_one = 1.0 - beta_one ** STEP
    correct_two = 1.0 - beta_two ** STEP
    moment_one_out = beta_one * moment_one + (1.0 - beta_one) * gradient
    moment_two_out = beta_two * moment_two + (1.0 - beta_two) * gradient * gradient
    update = moment_one_out / correct_one / (jnp.sqrt(moment_two_out / correct_two) + adam_eps)
    master_out = master - learn_rate * (update + decay_rate * master)
    ema_out = ema_decay * ema_weights + (1.0 - ema_decay) * master_out
    replicas = jnp.take(master_out, slot_expert.reshape(-1), axis=0).astype(jnp.bfloat16)
    return (master_out, moment_one_out, moment_two_out, ema_out, replicas)
```

```python
import functools

import jax
import jax.numpy as jnp
from jax import lax
from jax.experimental import pallas as pl
from jax.experimental.pallas import tpu as pltpu
from jax.sharding import PartitionSpec as P

STEP = 10


beta_one = 0.9
beta_two = 0.999
adam_eps = 1e-08
learn_rate = 0.05
decay_rate = 0.1
ema_decay = 0.99

MESH = pl.DeviceIdType.MESH
CORES = 2
VMEM_LIMIT = 42 * 1024 * 1024
CHUNKS = 7
AHEAD = 2
LAG = 4
DIRECT = 1


def row_tile(rows, most):
    return max(t for t in range(16, most + 1, 16) if rows % t == 0)


def adam(gradient, master, one, two):
    scale_one = 1.0 / (1.0 - beta_one**STEP)
    scale_two = 1.0 / (1.0 - beta_two**STEP)
    one_out = beta_one * one + (1.0 - beta_one) * gradient
    two_out = beta_two * two + (1.0 - beta_two) * gradient * gradient
    update = one_out * scale_one / (jnp.sqrt(two_out * scale_two) + adam_eps)
    return master - learn_rate * (update + decay_rate * master), one_out, two_out


def plan(chunks):
    order, updated = [], 0
    for c in range(min(AHEAD, chunks)):
        order.append(("reduce", c))
    for c in range(chunks):
        if c + AHEAD < chunks:
            order.append(("reduce", c + AHEAD))
        order.append(("own", c))
        if c >= LAG:
            order.append(("update", updated))
            updated += 1
    order += [("update", c) for c in range(updated, chunks)]
    order += [("forward", c) for c in range(chunks)]
    return order


def exchange_kernel(n_e, n_dp, chunks, cap, owner, slots, grad, master, one, two, ema,
                    master_out, one_out, two_out, ema_out, replicas, *refs):
    relayed = [c for c in range(chunks) if cap < n_e and c < chunks - DIRECT]
    refs = list(refs)

    def take(count):
        taken = refs[:count]
        del refs[:count]
        return taken

    gathered, slotted = take(chunks), take(chunks)
    cross, passed = take(len(relayed)), take(len(relayed))
    relay_near, relay_far = take(len(relayed)), take(len(relayed))
    (own, got, part, peer, done, held, rank, wanted_there,
     load_sem, pair_send, pair_recv, part_send, part_recv, out_send, out_recv, state_sem,
     same_send, same_recv, over_send, over_recv, cross_send, cross_recv, pass_send, pass_recv) = refs
    chips = n_dp // CORES
    rows, cols = master.shape[1], master.shape[2]
    size = rows // chunks
    width = replicas.shape[0]
    e = lax.axis_index("expert")
    d = lax.axis_index("dp")
    chip, core = d // CORES, d % CORES
    other = 1 - core
    half = n_e // 2
    side, place = e // half, e % half
    quarter = half // 2
    lane = place % quarter
    near = place // quarter == 1 - side
    tile = row_tile(size, 32)

    def relay_of(sender_side, sender_lane):
        there = 1 - sender_side
        return there * half + (1 - there) * quarter + sender_lane

    def remote(src, dst, send, recv, target):
        return pltpu.make_async_remote_copy(
            src_ref=src, dst_ref=dst, send_sem=send, recv_sem=recv, device_id=target, device_id_type=MESH)

    def columns(chip_of, core_of):
        return pl.ds(pl.multiple_of((chip_of * CORES + core_of) * cols, cols), cols)

    def chip_at(r):
        return lax.rem(chip + 1 + r, chips)

    def holder(k):
        return lax.rem(side + 1 - lax.rem(k, 2), 2) * half + lax.rem(place + lax.div(k + 1, 2), half)

    def rows_of(source, c):
        return pl.ds(pl.multiple_of(source * rows + c * size, size), size)

    def same_host(k):
        return side * half + lax.rem(place + 1 + k, half)

    def over_host(k):
        return (1 - side) * half + lax.rem(place + k, half)

    barrier = pltpu.get_barrier_semaphore()
    for r in range(1, n_dp):
        pl.semaphore_signal(barrier, inc=1, device_id=(e, lax.rem(d + r, n_dp)), device_id_type=MESH)
    for r in range(1, n_e):
        pl.semaphore_signal(barrier, inc=1, device_id=(lax.rem(e + r, n_e), d), device_id_type=MESH)

    loads, pairs = {}, {}
    for c in range(chunks):
        for r in range(chips):
            loads[c, r] = pltpu.make_async_copy(
                grad.at[:, c, :, columns(chip_at(r), core)], own.at[c, r], load_sem.at[c, r])
            loads[c, r].start()

    if relayed:
        def named(of_side):
            values = [slots[s, of_side * half + g] for g in range(half) for s in range(width)]
            flags = []
            for x in range(n_e):
                flag = jnp.int32(0)
                for value in values:
                    flag = jnp.maximum(flag, jnp.where(value == x, 1, 0))
                flags.append(flag)
            return flags

        count = jnp.int32(0)
        for x, flag in enumerate(named(side)):
            rank[x] = count
            count = count + flag
        flags = named(1 - side)
        for i in range(cap):
            count, chosen = jnp.int32(0), jnp.int32(0)
            for x in range(n_e):
                chosen = chosen + jnp.where(count == i, flags[x] * x, 0)
                count = count + flags[x]
            wanted_there[i] = chosen

    pl.semaphore_wait(barrier, n_dp - 1 + n_e - 1)
    for c in range(chunks):
        for r in range(chips):
            pairs[c, r] = remote(
                grad.at[:, c, :, columns(chip_at(r), other)], got.at[c, r],
                pair_send.at[c, r], pair_recv.at[c, r], (e, chip * CORES + other))
            pairs[c, r].start()
    states = [pltpu.make_async_copy(src, dst, state_sem.at[i]) for i, (src, dst) in
              enumerate(((master, master_out), (one, one_out), (two, two_out), (ema, ema_out)))]
    for copy in states:
        copy.start()

    def part_copy(c, k, r):
        return remote(part.at[c, k, r], peer.at[c, k, r], part_send.at[c, k, r], part_recv.at[c, k, r],
                      (e, chip_at(r) * CORES + core))

    def out_copy(c, k):
        return remote(done.at[c, k], gathered[c].at[e], out_send.at[c, k], out_recv.at[c, k], (holder(k), d))

    def same_copy(c, k):
        target = replicas.at[:, rows_of(e, c), :]
        if k == half - 1:
            return pltpu.make_async_copy(slotted[c].at[k], target, same_recv.at[c, k])
        return remote(slotted[c].at[k], target, same_send.at[c, k], same_recv.at[c, k], (same_host(k), d))

    def over_copy(c, k):
        return remote(slotted[c].at[half + k], replicas.at[:, rows_of(e, c), :],
                      over_send.at[c, k], over_recv.at[c, k], (over_host(k), d))

    def pass_rows(i, of_lane, c):
        return replicas.at[:, rows_of((1 - side) * half + i * quarter + of_lane, c), :]

    def pass_copy(c, i, k):
        target = pass_rows(i, lane, c)
        if k == half - 1:
            return pltpu.make_async_copy(passed[c].at[i, k], target, pass_recv.at[c, i, lane])
        return remote(passed[c].at[i, k], target, pass_send.at[c, i, k], pass_recv.at[c, i, lane], (same_host(k), d))

    def cross_copy(c, i):
        return remote(cross[c], (relay_near, relay_far)[i][c], cross_send.at[c], cross_recv.at[c, i],
                      (relay_of(side, lane), d))

    def tiles(body):
        @pl.loop(0, size // tile)
        def _(i):
            body(pl.ds(pl.multiple_of(i * tile, tile), tile))

    def reduce(c):
        for r in range(chips - 1):
            loads[c, r].wait()
            pairs[c, r].wait_recv()

        @pl.loop(0, n_e)
        def _(k):
            host = holder(k)
            for r in range(chips - 1):
                def add(at):
                    total = own[c, r, host, at, :].astype(jnp.float32) + got[c, r, host, at, :].astype(jnp.float32)
                    part[c, k, r, at, :] = total.astype(jnp.bfloat16)

                tiles(add)
                part_copy(c, k, r).start()

    def owned(c):
        last = chips - 1
        loads[c, last].wait()
        pairs[c, last].wait_recv()

        def summed(k, host, at):
            total = own[c, last, host, at, :].astype(jnp.float32) + got[c, last, host, at, :].astype(jnp.float32)
            for r in range(chips - 1):
                total = total + peer[c, k, r, at, :].astype(jnp.float32)
            return total.astype(jnp.bfloat16)

        @pl.loop(0, n_e - 1)
        def _(k):
            for r in range(chips - 1):
                part_copy(c, k, r).wait_recv()

            def add(at):
                done[c, k, at, :] = summed(k, holder(k), at)

            tiles(add)
            out_copy(c, k).start()

        for r in range(chips - 1):
            part_copy(c, n_e - 1, r).wait_recv()

        def keep(at):
            gathered[c][e, at, :] = summed(n_e - 1, e, at)

        tiles(keep)

    def update(c):
        if c == 0:
            for copy in states:
                copy.wait()

        @pl.loop(0, n_e - 1)
        def _(k):
            out_copy(c, k).wait_recv()

        @pl.loop(0, n_e)
        def _(x):
            position = owner[x]

            @pl.loop(0, size // tile)
            def _(i):
                at = pl.ds(pl.multiple_of(i * tile, tile), tile)
                there = pl.ds(pl.multiple_of(c * size + i * tile, tile), tile)
                gradient = gathered[c][position, at, :].astype(jnp.float32)
                new, first, second = adam(
                    gradient, master_out[x, there, :], one_out[x, there, :], two_out[x, there, :])
                held[x, at, :] = new.astype(jnp.bfloat16)
                master_out[x, there, :] = new
                one_out[x, there, :] = first
                two_out[x, there, :] = second

        if c in relayed:
            @pl.loop(0, cap)
            def _(i):
                wanted = wanted_there[i]

                def pick(at):
                    cross[c][i, at, :] = held[wanted, at, :]

                tiles(pick)

            for i in range(2):
                @pl.when(place // quarter == i)
                def _():
                    cross_copy(c, i).start()
        else:
            for k in range(half):
                for s in range(width):
                    wanted = slots[s, over_host(k)]

                    def pick(at):
                        slotted[c][half + k, s, at, :] = held[wanted, at, :]

                    tiles(pick)
                over_copy(c, k).start()

        for k in range(half):
            for s in range(width):
                wanted = slots[s, same_host(k)]

                def pick(at):
                    slotted[c][k, s, at, :] = held[wanted, at, :]

                tiles(pick)
            same_copy(c, k).start()

        @pl.loop(0, n_e)
        def _(x):
            @pl.loop(0, size // tile)
            def _(i):
                there = pl.ds(pl.multiple_of(c * size + i * tile, tile), tile)
                ema_out[x, there, :] = (
                    ema_decay * ema_out[x, there, :] + (1.0 - ema_decay) * master_out[x, there, :])

    def forward(c):
        if c not in relayed:
            return

        @pl.when(near)
        def _():
            for i in range(2):
                cross_copy(c, i).wait_recv()
                arrived = (relay_near, relay_far)[i][c]
                for k in range(half):
                    for s in range(width):
                        position = rank[slots[s, same_host(k)]]

                        def pick(at):
                            passed[c][i, k, s, at, :] = arrived[position, at, :]

                        tiles(pick)
                    pass_copy(c, i, k).start()

    stages = {"reduce": reduce, "own": owned, "update": update, "forward": forward}
    for stage, c in plan(chunks):
        stages[stage](c)

    for c in range(chunks):
        for r in range(chips):
            pairs[c, r].wait_send()

        @pl.loop(0, n_e)
        def _(k):
            for r in range(chips - 1):
                part_copy(c, k, r).wait_send()

        @pl.loop(0, n_e - 1)
        def _(k):
            out_copy(c, k).wait_send()

        for k in range(half):
            same_copy(c, k).wait()
        if c in relayed:
            cross_copy(c, 0).wait_send()

            @pl.when(near)
            def _():
                for i in range(2):
                    for k in range(half - 1):
                        pass_copy(c, i, k).wait_send()

            for i in range(2):
                for r in range(quarter):
                    remote(passed[c].at[i, 0], pass_rows(i, r, c), pass_send.at[c, i, 0], pass_recv.at[c, i, r],
                           (same_host(0), d)).wait_recv()
        else:
            for k in range(half):
                over_copy(c, k).wait()


def write_kernel(*refs):
    count = len(refs) // 2
    sem = refs[-1]
    copies = [pltpu.make_async_copy(refs[i], refs[count + i], sem.at[i]) for i in range(count)]
    for copy in copies:
        copy.start()
    for copy in copies:
        copy.wait()


def written(arrays):
    hbm = pl.BlockSpec(memory_space=pl.ANY)
    return pl.pallas_call(
        write_kernel,
        out_shape=[jax.ShapeDtypeStruct(a.shape, a.dtype) for a in arrays],
        in_specs=[hbm] * len(arrays),
        out_specs=[hbm] * len(arrays),
        scratch_shapes=[pltpu.SemaphoreType.DMA((len(arrays),))],
        compiler_params=pltpu.CompilerParams(vmem_limit_bytes=1024 * 1024),
        name="write",
    )(*[pltpu.with_memory_space_constraint(a, pltpu.VMEM) for a in arrays])


def exchanged(n_e, n_dp, cap, number, grad, owner_slot, slot_expert, master, one, two, ema):
    rows, cols = master.shape[1], master.shape[2]
    chips = n_dp // CORES
    width = slot_expert.shape[1]
    chunks = CHUNKS
    size = rows // chunks
    side = n_e // 2
    relayed = chunks - DIRECT if cap < n_e else 0
    dma = pltpu.SemaphoreType.DMA
    half = jnp.bfloat16
    hbm = pl.BlockSpec(memory_space=pl.ANY)
    vmem = pl.BlockSpec(memory_space=pltpu.VMEM)
    smem = pl.BlockSpec(memory_space=pltpu.SMEM)
    return pl.pallas_call(
        functools.partial(exchange_kernel, n_e, n_dp, chunks, cap),
        out_shape=[pltpu.VMEM(master.shape, jnp.float32)] * 4 + [pltpu.VMEM((width, n_e * rows, cols), half)],
        in_specs=[smem, smem] + [hbm] * 5,
        out_specs=[vmem] * 5,
        scratch_shapes=[pltpu.VMEM((n_e, size, cols), half)] * chunks
        + [pltpu.VMEM((side if c < relayed else n_e, width, size, cols), half) for c in range(chunks)]
        + [pltpu.VMEM((cap, size, cols), half)] * relayed
        + [pltpu.VMEM((2, side, width, size, cols), half)] * relayed
        + [pltpu.VMEM((cap, size, cols), half)] * (2 * relayed)
        + [
            pltpu.VMEM((chunks, chips, n_e, size, cols), half),
            pltpu.VMEM((chunks, chips, n_e, size, cols), half),
            pltpu.VMEM((chunks, n_e, chips - 1, size, cols), half),
            pltpu.VMEM((chunks, n_e, chips - 1, size, cols), half),
            pltpu.VMEM((chunks, n_e, size, cols), half),
            pltpu.VMEM((n_e, size, cols), half),
            pltpu.SMEM((n_e,), jnp.int32),
            pltpu.SMEM((n_e,), jnp.int32),
            dma((chunks, chips)),
            dma((chunks, chips)),
            dma((chunks, chips)),
            dma((chunks, n_e, chips - 1)),
            dma((chunks, n_e, chips - 1)),
            dma((chunks, n_e)),
            dma((chunks, n_e)),
            dma((4,)),
            dma((chunks, side)),
            dma((chunks, side)),
            dma((chunks, side)),
            dma((chunks, side)),
            dma((chunks,)),
            dma((chunks, 2)),
            dma((chunks, 2, side)),
            dma((chunks, 2, side // 2)),
        ],
        compiler_params=pltpu.CompilerParams(
            collective_id=number, has_side_effects=True, vmem_limit_bytes=VMEM_LIMIT),
        name=f"exchange_{cap}",
    )(owner_slot, slot_expert.T, grad.reshape(n_e, chunks, size, grad.shape[-1]), master, one, two, ema)


def per_device(n_e, n_dp, grad_parts, owner_slot, slot_expert, master, moment_one, moment_two, ema_weights):
    side = n_e // 2
    caps = sorted({n_e - n_e // 4, n_e - n_e // 8, n_e})
    hosts = lax.broadcasted_iota(jnp.int32, slot_expert.shape, 0)
    bits = jnp.left_shift(jnp.uint32(1), (slot_expert + n_e * (hosts // side)).astype(jnp.uint32))
    mask = lax.reduce(bits, jnp.uint32(0), lax.bitwise_or, (0, 1))
    first = lax.population_count(mask & jnp.uint32(2**n_e - 1))
    second = lax.population_count(mask >> n_e)
    distinct = jnp.maximum(first, second).astype(jnp.int32)
    branch = sum((distinct > cap).astype(jnp.int32) for cap in caps[:-1])
    branches = [
        lambda *arrays, cap=cap, number=number: tuple(written(exchanged(n_e, n_dp, cap, number, *arrays)))
        for number, cap in enumerate(caps)]
    return lax.switch(
        branch, branches,
        grad_parts[0, 0], owner_slot, slot_expert, master, moment_one, moment_two, ema_weights)


def solution(mesh):
    placed = (
        P("dp", "expert", None, None),
        P(),
        P(),
        P(None, "expert", "dp"),
        P(None, "expert", "dp"),
        P(None, "expert", "dp"),
        P(None, "expert", "dp"),
    )
    return jax.shard_map(
        functools.partial(per_device, mesh.shape["expert"], mesh.shape["dp"]),
        mesh=mesh,
        in_specs=placed,
        out_specs=(
            P(None, "expert", "dp"),
            P(None, "expert", "dp"),
            P(None, "expert", "dp"),
            P(None, "expert", "dp"),
            P("expert", None, "dp"),
        ),
        check_vma=False,
    )
```

```python
import functools

import jax
import jax.numpy as jnp
from jax import lax
from jax.experimental import pallas as pl
from jax.experimental.pallas import tpu as pltpu
from jax.sharding import PartitionSpec as P

STEP = 10


beta_one = 0.9
beta_two = 0.999
adam_eps = 1e-08
learn_rate = 0.05
decay_rate = 0.1
ema_decay = 0.99

MESH = pl.DeviceIdType.MESH
CORES = 2
VMEM_LIMIT = 42 * 1024 * 1024
CHUNKS = 7
AHEAD = 2
LAG = 1
BEHIND = 1
DIRECT = 2


def row_tile(rows, most):
    return max(t for t in range(16, most + 1, 16) if rows % t == 0)


def adam(gradient, master, one, two):
    scale_one = 1.0 / (1.0 - beta_one**STEP)
    scale_two = 1.0 / (1.0 - beta_two**STEP)
    one_out = beta_one * one + (1.0 - beta_one) * gradient
    two_out = beta_two * two + (1.0 - beta_two) * gradient * gradient
    update = one_out * scale_one / (jnp.sqrt(two_out * scale_two) + adam_eps)
    return master - learn_rate * (update + decay_rate * master), one_out, two_out


def plan(chunks):
    order = [("reduce", c) for c in range(min(AHEAD, chunks))]
    for t in range(chunks + LAG + BEHIND):
        for stage, c in (("reduce", t + AHEAD), ("own", t), ("update", t - LAG), ("forward", t - LAG - BEHIND)):
            if 0 <= c < chunks and (stage, c) not in order:
                order.append((stage, c))
    return order


def exchange_kernel(n_e, n_dp, chunks, cap, owner, slots, grad, master, one, two, ema,
                    master_out, one_out, two_out, ema_out, replicas, *refs):
    relayed = [c for c in range(chunks) if cap < n_e and c < chunks - DIRECT]
    refs = list(refs)

    def take(count):
        taken = refs[:count]
        del refs[:count]
        return taken

    gathered, slotted = take(chunks), take(chunks)
    cross, passed = take(len(relayed)), take(len(relayed))
    relay_near, relay_far = take(len(relayed)), take(len(relayed))
    (own, got, part, peer, done, held, rank, wanted_there,
     load_sem, pair_send, pair_recv, part_send, part_recv, out_send, out_recv, state_sem,
     same_send, same_recv, over_send, over_recv, cross_send, cross_recv, pass_send, pass_recv) = refs
    chips = n_dp // CORES
    rows, cols = master.shape[1], master.shape[2]
    size = rows // chunks
    width = replicas.shape[0]
    e = lax.axis_index("expert")
    d = lax.axis_index("dp")
    chip, core = d // CORES, d % CORES
    other = 1 - core
    half = n_e // 2
    side, place = e // half, e % half
    quarter = half // 2
    lane = place % quarter
    near = place // quarter == 1 - side
    tile = row_tile(size, 32)

    def relay_of(sender_side, sender_lane):
        there = 1 - sender_side
        return there * half + (1 - there) * quarter + sender_lane

    def remote(src, dst, send, recv, target):
        return pltpu.make_async_remote_copy(
            src_ref=src, dst_ref=dst, send_sem=send, recv_sem=recv, device_id=target, device_id_type=MESH)

    def columns(chip_of, core_of):
        return pl.ds(pl.multiple_of((chip_of * CORES + core_of) * cols, cols), cols)

    def chip_at(r):
        return lax.rem(chip + 1 + r, chips)

    def holder(k):
        return lax.rem(side + 1 - lax.rem(k, 2), 2) * half + lax.rem(place + lax.div(k + 1, 2), half)

    def rows_of(source, c):
        return pl.ds(pl.multiple_of(source * rows + c * size, size), size)

    def same_host(k):
        return side * half + lax.rem(place + 1 + k, half)

    def over_host(k):
        return (1 - side) * half + lax.rem(place + k, half)

    barrier = pltpu.get_barrier_semaphore()
    for r in range(1, n_dp):
        pl.semaphore_signal(barrier, inc=1, device_id=(e, lax.rem(d + r, n_dp)), device_id_type=MESH)
    for r in range(1, n_e):
        pl.semaphore_signal(barrier, inc=1, device_id=(lax.rem(e + r, n_e), d), device_id_type=MESH)

    loads, pairs = {}, {}
    for c in range(chunks):
        for r in range(chips):
            loads[c, r] = pltpu.make_async_copy(
                grad.at[:, c, :, columns(chip_at(r), core)], own.at[c, r], load_sem.at[c, r])
            loads[c, r].start()

    if relayed:
        def named(of_side):
            values = [slots[s, of_side * half + g] for g in range(half) for s in range(width)]
            flags = []
            for x in range(n_e):
                flag = jnp.int32(0)
                for value in values:
                    flag = jnp.maximum(flag, jnp.where(value == x, 1, 0))
                flags.append(flag)
            return flags

        count = jnp.int32(0)
        for x, flag in enumerate(named(side)):
            rank[x] = count
            count = count + flag
        flags = named(1 - side)
        for i in range(cap):
            count, chosen = jnp.int32(0), jnp.int32(0)
            for x in range(n_e):
                chosen = chosen + jnp.where(count == i, flags[x] * x, 0)
                count = count + flags[x]
            wanted_there[i] = chosen

    pl.semaphore_wait(barrier, n_dp - 1 + n_e - 1)
    for c in range(chunks):
        for r in range(chips):
            pairs[c, r] = remote(
                grad.at[:, c, :, columns(chip_at(r), other)], got.at[c, r],
                pair_send.at[c, r], pair_recv.at[c, r], (e, chip * CORES + other))
            pairs[c, r].start()
    states = [pltpu.make_async_copy(src, dst, state_sem.at[i]) for i, (src, dst) in
              enumerate(((master, master_out), (one, one_out), (two, two_out), (ema, ema_out)))]
    for copy in states:
        copy.start()

    def part_copy(c, k, r):
        return remote(part.at[c, k, r], peer.at[c, k, r], part_send.at[c, k, r], part_recv.at[c, k, r],
                      (e, chip_at(r) * CORES + core))

    def out_copy(c, k):
        return remote(done.at[c, k], gathered[c].at[e], out_send.at[c, k], out_recv.at[c, k], (holder(k), d))

    def same_copy(c, k):
        target = replicas.at[:, rows_of(e, c), :]
        if k == half - 1:
            return pltpu.make_async_copy(slotted[c].at[k], target, same_recv.at[c, k])
        return remote(slotted[c].at[k], target, same_send.at[c, k], same_recv.at[c, k], (same_host(k), d))

    def over_copy(c, k):
        return remote(slotted[c].at[half + k], replicas.at[:, rows_of(e, c), :],
                      over_send.at[c, k], over_recv.at[c, k], (over_host(k), d))

    def pass_rows(i, of_lane, c):
        return replicas.at[:, rows_of((1 - side) * half + i * quarter + of_lane, c), :]

    def pass_copy(c, i, k):
        target = pass_rows(i, lane, c)
        if k == half - 1:
            return pltpu.make_async_copy(passed[c].at[i, k], target, pass_recv.at[c, i, lane])
        return remote(passed[c].at[i, k], target, pass_send.at[c, i, k], pass_recv.at[c, i, lane], (same_host(k), d))

    def cross_copy(c, i):
        return remote(cross[c], (relay_near, relay_far)[i][c], cross_send.at[c], cross_recv.at[c, i],
                      (relay_of(side, lane), d))

    def tiles(body):
        @pl.loop(0, size // tile)
        def _(i):
            body(pl.ds(pl.multiple_of(i * tile, tile), tile))

    def reduce(c):
        for r in range(chips - 1):
            loads[c, r].wait()
            pairs[c, r].wait_recv()

        @pl.loop(0, n_e)
        def _(k):
            host = holder(k)
            for r in range(chips - 1):
                def add(at):
                    total = own[c, r, host, at, :].astype(jnp.float32) + got[c, r, host, at, :].astype(jnp.float32)
                    part[c, k, r, at, :] = total.astype(jnp.bfloat16)

                tiles(add)
                part_copy(c, k, r).start()

    def owned(c):
        last = chips - 1
        loads[c, last].wait()
        pairs[c, last].wait_recv()

        def summed(k, host, at):
            total = own[c, last, host, at, :].astype(jnp.float32) + got[c, last, host, at, :].astype(jnp.float32)
            for r in range(chips - 1):
                total = total + peer[c, k, r, at, :].astype(jnp.float32)
            return total.astype(jnp.bfloat16)

        @pl.loop(0, n_e - 1)
        def _(k):
            for r in range(chips - 1):
                part_copy(c, k, r).wait_recv()

            def add(at):
                done[c, k, at, :] = summed(k, holder(k), at)

            tiles(add)
            out_copy(c, k).start()

        for r in range(chips - 1):
            part_copy(c, n_e - 1, r).wait_recv()

        def keep(at):
            gathered[c][e, at, :] = summed(n_e - 1, e, at)

        tiles(keep)

    def update(c):
        if c == 0:
            for copy in states:
                copy.wait()

        @pl.loop(0, n_e - 1)
        def _(k):
            out_copy(c, k).wait_recv()

        @pl.loop(0, n_e)
        def _(x):
            position = owner[x]

            @pl.loop(0, size // tile)
            def _(i):
                at = pl.ds(pl.multiple_of(i * tile, tile), tile)
                there = pl.ds(pl.multiple_of(c * size + i * tile, tile), tile)
                gradient = gathered[c][position, at, :].astype(jnp.float32)
                new, first, second = adam(
                    gradient, master_out[x, there, :], one_out[x, there, :], two_out[x, there, :])
                held[x, at, :] = new.astype(jnp.bfloat16)
                master_out[x, there, :] = new
                one_out[x, there, :] = first
                two_out[x, there, :] = second

        if c in relayed:
            @pl.loop(0, cap)
            def _(i):
                wanted = wanted_there[i]

                def pick(at):
                    cross[c][i, at, :] = held[wanted, at, :]

                tiles(pick)

            for i in range(2):
                @pl.when(place // quarter == i)
                def _():
                    cross_copy(c, i).start()
        else:
            for k in range(half):
                for s in range(width):
                    wanted = slots[s, over_host(k)]

                    def pick(at):
                        slotted[c][half + k, s, at, :] = held[wanted, at, :]

                    tiles(pick)
                over_copy(c, k).start()

        for k in range(half):
            for s in range(width):
                wanted = slots[s, same_host(k)]

                def pick(at):
                    slotted[c][k, s, at, :] = held[wanted, at, :]

                tiles(pick)
            same_copy(c, k).start()

        @pl.loop(0, n_e)
        def _(x):
            @pl.loop(0, size // tile)
            def _(i):
                there = pl.ds(pl.multiple_of(c * size + i * tile, tile), tile)
                ema_out[x, there, :] = (
                    ema_decay * ema_out[x, there, :] + (1.0 - ema_decay) * master_out[x, there, :])

    def forward(c):
        if c not in relayed:
            return

        @pl.when(near)
        def _():
            for i in range(2):
                cross_copy(c, i).wait_recv()
                arrived = (relay_near, relay_far)[i][c]
                for k in range(half):
                    for s in range(width):
                        position = rank[slots[s, same_host(k)]]

                        def pick(at):
                            passed[c][i, k, s, at, :] = arrived[position, at, :]

                        tiles(pick)
                    pass_copy(c, i, k).start()

    stages = {"reduce": reduce, "own": owned, "update": update, "forward": forward}
    for stage, c in plan(chunks):
        stages[stage](c)

    for c in range(chunks):
        for r in range(chips):
            pairs[c, r].wait_send()

        @pl.loop(0, n_e)
        def _(k):
            for r in range(chips - 1):
                part_copy(c, k, r).wait_send()

        @pl.loop(0, n_e - 1)
        def _(k):
            out_copy(c, k).wait_send()

        for k in range(half):
            same_copy(c, k).wait()
        if c in relayed:
            cross_copy(c, 0).wait_send()

            @pl.when(near)
            def _():
                for i in range(2):
                    for k in range(half - 1):
                        pass_copy(c, i, k).wait_send()

            for i in range(2):
                for r in range(quarter):
                    remote(passed[c].at[i, 0], pass_rows(i, r, c), pass_send.at[c, i, 0], pass_recv.at[c, i, r],
                           (same_host(0), d)).wait_recv()
        else:
            for k in range(half):
                over_copy(c, k).wait()


def write_kernel(*refs):
    count = len(refs) // 2
    sem = refs[-1]
    copies = [pltpu.make_async_copy(refs[i], refs[count + i], sem.at[i]) for i in range(count)]
    for copy in copies:
        copy.start()
    for copy in copies:
        copy.wait()


def written(arrays):
    hbm = pl.BlockSpec(memory_space=pl.ANY)
    return pl.pallas_call(
        write_kernel,
        out_shape=[jax.ShapeDtypeStruct(a.shape, a.dtype) for a in arrays],
        in_specs=[hbm] * len(arrays),
        out_specs=[hbm] * len(arrays),
        scratch_shapes=[pltpu.SemaphoreType.DMA((len(arrays),))],
        compiler_params=pltpu.CompilerParams(vmem_limit_bytes=1024 * 1024),
        name="write",
    )(*[pltpu.with_memory_space_constraint(a, pltpu.VMEM) for a in arrays])


def exchanged(n_e, n_dp, cap, number, grad, owner_slot, slot_expert, master, one, two, ema):
    rows, cols = master.shape[1], master.shape[2]
    chips = n_dp // CORES
    width = slot_expert.shape[1]
    chunks = CHUNKS
    size = rows // chunks
    side = n_e // 2
    relayed = chunks - DIRECT if cap < n_e else 0
    dma = pltpu.SemaphoreType.DMA
    half = jnp.bfloat16
    hbm = pl.BlockSpec(memory_space=pl.ANY)
    vmem = pl.BlockSpec(memory_space=pltpu.VMEM)
    smem = pl.BlockSpec(memory_space=pltpu.SMEM)
    return pl.pallas_call(
        functools.partial(exchange_kernel, n_e, n_dp, chunks, cap),
        out_shape=[pltpu.VMEM(master.shape, jnp.float32)] * 4 + [pltpu.VMEM((width, n_e * rows, cols), half)],
        in_specs=[smem, smem] + [hbm] * 5,
        out_specs=[vmem] * 5,
        scratch_shapes=[pltpu.VMEM((n_e, size, cols), half)] * chunks
        + [pltpu.VMEM((side if c < relayed else n_e, width, size, cols), half) for c in range(chunks)]
        + [pltpu.VMEM((cap, size, cols), half)] * relayed
        + [pltpu.VMEM((2, side, width, size, cols), half)] * relayed
        + [pltpu.VMEM((cap, size, cols), half)] * (2 * relayed)
        + [
            pltpu.VMEM((chunks, chips, n_e, size, cols), half),
            pltpu.VMEM((chunks, chips, n_e, size, cols), half),
            pltpu.VMEM((chunks, n_e, chips - 1, size, cols), half),
            pltpu.VMEM((chunks, n_e, chips - 1, size, cols), half),
            pltpu.VMEM((chunks, n_e, size, cols), half),
            pltpu.VMEM((n_e, size, cols), half),
            pltpu.SMEM((n_e,), jnp.int32),
            pltpu.SMEM((n_e,), jnp.int32),
            dma((chunks, chips)),
            dma((chunks, chips)),
            dma((chunks, chips)),
            dma((chunks, n_e, chips - 1)),
            dma((chunks, n_e, chips - 1)),
            dma((chunks, n_e)),
            dma((chunks, n_e)),
            dma((4,)),
            dma((chunks, side)),
            dma((chunks, side)),
            dma((chunks, side)),
            dma((chunks, side)),
            dma((chunks,)),
            dma((chunks, 2)),
            dma((chunks, 2, side)),
            dma((chunks, 2, side // 2)),
        ],
        compiler_params=pltpu.CompilerParams(
            collective_id=number, has_side_effects=True, vmem_limit_bytes=VMEM_LIMIT),
        name=f"exchange_{cap}",
    )(owner_slot, slot_expert.T, grad.reshape(n_e, chunks, size, grad.shape[-1]), master, one, two, ema)


def per_device(n_e, n_dp, grad_parts, owner_slot, slot_expert, master, moment_one, moment_two, ema_weights):
    side = n_e // 2
    caps = sorted({n_e - n_e // 4, n_e - n_e // 8, n_e})
    hosts = lax.broadcasted_iota(jnp.int32, slot_expert.shape, 0)
    bits = jnp.left_shift(jnp.uint32(1), (slot_expert + n_e * (hosts // side)).astype(jnp.uint32))
    mask = lax.reduce(bits, jnp.uint32(0), lax.bitwise_or, (0, 1))
    first = lax.population_count(mask & jnp.uint32(2**n_e - 1))
    second = lax.population_count(mask >> n_e)
    distinct = jnp.maximum(first, second).astype(jnp.int32)
    branch = sum((distinct > cap).astype(jnp.int32) for cap in caps[:-1])
    branches = [
        lambda *arrays, cap=cap, number=number: tuple(written(exchanged(n_e, n_dp, cap, number, *arrays)))
        for number, cap in enumerate(caps)]
    return lax.switch(
        branch, branches,
        grad_parts[0, 0], owner_slot, slot_expert, master, moment_one, moment_two, ema_weights)


def solution(mesh):
    placed = (
        P("dp", "expert", None, None),
        P(),
        P(),
        P(None, "expert", "dp"),
        P(None, "expert", "dp"),
        P(None, "expert", "dp"),
        P(None, "expert", "dp"),
    )
    return jax.shard_map(
        functools.partial(per_device, mesh.shape["expert"], mesh.shape["dp"]),
        mesh=mesh,
        in_specs=placed,
        out_specs=(
            P(None, "expert", "dp"),
            P(None, "expert", "dp"),
            P(None, "expert", "dp"),
            P(None, "expert", "dp"),
            P("expert", None, "dp"),
        ),
        check_vma=False,
    )
```
